256 devices in a mesh: blk: 8 (over x_lo, y), freq: 32 (over x_hi, z, core).
Axes of the slice: x: 4 (x_hi: 2, x_lo: 2; x = x_hi * 2 + x_lo), y: 4, z: 8, core: 2. Of those that a mesh axis runs over, the one named last changes fastest.
Arguments:
- spectra: bfloat16 [2048, 2, 4096], P('blk', None, 'freq'), may hold values from -180 to 180
- pair_first: int32 [8, 8, 2048], P('blk'), may hold values from 0 to 255
- pair_second: int32 [8, 8, 2048], P('blk'), may hold values from 0 to 255
- pair_bin: int32 [8, 8, 2048], P('blk'), may hold values from 0 to 63, as said below
- bin_owner: int32 [64], replicated, may hold values from 0 to 7, as said below
Outputs:
- correlation: float32 [4096, 128], P('freq', 'blk')
The draws below stay inside these ranges and needn't reach their ends.
Inputs may be any that keep to these rules, and one draw needn't show every extreme that they name: Each list pair_bin[a, r] is nondecreasing along its last dimension, starts with 0 and ends with 63. `bin_owner`: each block index owns at most 16 bins, and some index owns exactly 16.
All inputs are finite; a program needn't handle non-finite values.
Results may differ from the reference program's by a relative error of at most 0.0049.
Values may be sent and summed in bfloat16 or wider, within the bound.
No kernel may reach another device: no remote copies, remote signals or barrier semaphores. Data moves between devices by JAX's collectives and lax.ppermute only.
A program may use at most 64 MiB of HBM per device.

```python
import math
import jax
import jax.numpy as jnp
from jax import lax

S_DEV = 256
F = 4096
NB = 64
PAIRS = 2048
BLOCKS = 8
SENSORS = 2048
SLOTS = 128
BMAX = 16


def draw_spectra(key, part):
    keys = jax.random.split(key, 3)
    sensor_scale = jnp.exp(jax.random.uniform(keys[0], (SENSORS, 1, 1), jnp.float32, 0.0, math.log(10.0)))
    bins = jnp.arange(F, dtype=jnp.float32) / F
    freq_scale = jnp.exp(bins * math.log(3.0))[None, None, :]
    freq_scale = freq_scale * jnp.exp(jax.random.uniform(keys[1], (1, 1, F), jnp.float32, -0.35, 0.35))
    base = jnp.clip(jax.random.normal(keys[2], (SENSORS, 2, F), jnp.float32), -4.0, 4.0)
    return (base * sensor_scale * freq_scale).astype(jnp.bfloat16)


def draw_pair_bin(key, part):
    values = jax.random.randint(key, (BLOCKS, BLOCKS, PAIRS), 0, NB, jnp.int32)
    values = values.at[:, :, 0].set(0)
    values = values.at[:, :, PAIRS - 1].set(NB - 1)
    return jnp.sort(values, axis=-1)


def draw_bin_owner(key, part):
    keys = jax.random.split(jax.random.fold_in(key, 7), 2)
    order = jax.random.permutation(keys[0], NB)
    busiest = jax.random.randint(keys[1], (), 0, BLOCKS, jnp.int32)
    place = jnp.arange(NB, dtype=jnp.int32)
    others = max(BLOCKS - 1, 1)
    owner_of_place = jnp.where(place < BMAX, busiest, (busiest + 1 + (place - BMAX) % others) % BLOCKS)
    return jnp.zeros((NB,), jnp.int32).at[order].set(owner_of_place.astype(jnp.int32))


def set_ends(array, stream_key, smallest, top_value):
    dims = array.shape
    spot = [jax.random.randint(jax.random.fold_in(stream_key, axis), (), 0, dims[axis]) for axis in range(len(dims))]
    array = array.at[tuple(spot)].set(smallest)
    longest = dims.index(max(dims))
    spot[longest] = (spot[longest] + 1) % dims[longest]
    return array.at[tuple(spot)].set(top_value)


def setup_inputs(seed: int = 0) -> dict:
    key_list = jax.random.split(jax.random.key(seed), 6)
    spectra = draw_spectra(jax.random.fold_in(key_list[5], 71), 0)
    pair_first = set_ends(jax.random.randint(key_list[1], (BLOCKS, BLOCKS, PAIRS), 0, S_DEV), jax.random.fold_in(key_list[1], 1), 0, S_DEV - 1).astype(jnp.int32)
    pair_second = set_ends(jax.random.randint(key_list[2], (BLOCKS, BLOCKS, PAIRS), 0, S_DEV), jax.random.fold_in(key_list[2], 1), 0, S_DEV - 1).astype(jnp.int32)
    pair_bin = draw_pair_bin(jax.random.fold_in(key_list[5], 71), 0)
    bin_owner = draw_bin_owner(jax.random.fold_in(key_list[5], 71), 0)
    return dict(spectra=spectra, pair_first=pair_first, pair_second=pair_second, pair_bin=pair_bin, bin_owner=bin_owner)


def reference(spectra, pair_first, pair_second, pair_bin, bin_owner):
    x = spectra.astype(jnp.float32)
    power = lax.optimization_barrier(jnp.sum(x * x, axis=(1, 2)))
    rms = jnp.sqrt(power / (2 * F) + 1e-06)
    white = (x / rms[:, None, None]).astype(jnp.bfloat16)

    def one_list(total, index):
        first_block = index // BLOCKS
        step_count = index % BLOCKS
        other_block = (first_block - step_count) % BLOCKS
        rows_one = pair_first[first_block, step_count] + first_block * S_DEV
        rows_two = pair_second[first_block, step_count] + other_block * S_DEV
        left = white[rows_one].astype(jnp.float32)
        right = white[rows_two].astype(jnp.float32)
        real_part = left[:, 0] * right[:, 0] + left[:, 1] * right[:, 1]
        imag_part = left[:, 1] * right[:, 0] - left[:, 0] * right[:, 1]
        cross = jnp.stack([real_part, imag_part], 1).astype(jnp.bfloat16)
        cross = lax.optimization_barrier(cross).astype(jnp.float32)
        total = total + jax.ops.segment_sum(cross, pair_bin[first_block, step_count], NB)
        return (total, 0)
    start = jnp.zeros((NB, 2, F), jnp.float32)
    stack, unused = lax.scan(one_list, start, jnp.arange(BLOCKS * BLOCKS, dtype=jnp.int32))
    lags = jnp.arange(F, dtype=jnp.int32)
    phase = (lags[:, None] * lags[None, :] % F).astype(jnp.float32) * (2.0 * math.pi / F)
    line = jnp.dot(jnp.cos(phase), stack[:, 0, :].T, precision=lax.Precision.HIGHEST)
    line = line - jnp.dot(jnp.sin(phase), stack[:, 1, :].T, precision=lax.Precision.HIGHEST)
    scale = (F * PAIRS * BLOCKS * BLOCKS / NB) ** (-0.5)
    line = line * scale
    bins = jnp.arange(NB, dtype=jnp.int32)
    same = bin_owner[:, None] == bin_owner[None, :]
    lower = bins[None, :] < bins[:, None]
    rank = lax.optimization_barrier(jnp.sum((same & lower).astype(jnp.int32), axis=1)).astype(jnp.int32)
    slot = bin_owner * BMAX + rank
    return jnp.zeros((F, SLOTS), jnp.float32).at[:, slot].set(line)
```

```python
import math

import jax
import jax.numpy as jnp
from jax import lax
from jax.experimental import pallas as pl
from jax.experimental.pallas import tpu as pltpu
from jax.sharding import PartitionSpec as P

F = 4096
NB = 64
PAIRS = 2048
CHUNK = 256
CHUNKS = PAIRS // CHUNK
F32 = jnp.float32
BF16 = jnp.bfloat16
VMEM = pl.BlockSpec(memory_space=pltpu.VMEM)
SMEM = pl.BlockSpec(memory_space=pltpu.SMEM)


def shape(dims, dtype):
    return jax.ShapeDtypeStruct(dims, dtype)


def cost(flops, moved):
    return pl.CostEstimate(flops=flops, bytes_accessed=moved, transcendentals=0)


def split(x):
    hi = x.astype(BF16)
    return hi, (x - hi.astype(F32)).astype(BF16)


def power_kernel(x_ref, out_ref):
    x = x_ref[...].astype(F32)
    part = jnp.sum(x * x, axis=0, keepdims=True)
    out_ref[...] = jnp.broadcast_to(part[None], out_ref.shape)


def factors_kernel(me_ref, owner_row_ref, owner_col_ref, part_ref, hi_ref, lo_ref, select_ref):
    n = 128
    j = lax.broadcasted_iota(jnp.int32, (n, n), 0)
    i = lax.broadcasted_iota(jnp.int32, (n, n), 1)
    unit = 2.0 * math.pi / F
    first = ((i * (me_ref[0] * n + j)) % F).astype(F32) * unit
    step = ((n * j) % F).astype(F32) * unit
    re, im = jnp.cos(first), jnp.sin(first)
    sr, si = jnp.cos(step), jnp.sin(step)
    for block in range(F // n):
        lanes = pl.ds(block * n, n)
        hi, lo = split(re)
        hi_ref[:n, lanes] = hi
        lo_ref[:n, lanes] = lo
        hi, lo = split(-im)
        hi_ref[n:, lanes] = hi
        lo_ref[n:, lanes] = lo
        re, im = re * sr - im * si, re * si + im * sr
    row, col = owner_row_ref[...], owner_col_ref[...]
    b2 = lax.broadcasted_iota(jnp.int32, (NB, NB), 0)
    b = lax.broadcasted_iota(jnp.int32, (NB, NB), 1)
    ahead = jnp.where((col == row) & (b2 < b), 1.0, 0.0)
    rank = jnp.sum(ahead, axis=0, keepdims=True)
    slots = select_ref.shape[0]
    slot = row.astype(F32) * (slots // 8) + rank
    place = lax.broadcasted_iota(jnp.int32, (slots, NB), 0).astype(F32)
    select_ref[...] = jnp.where(place == slot, 1.0, 0.0).astype(BF16)


def white_kernel(parts_ref, x_ref, lists_ref, own_ref, *sent):
    power = jnp.sum(parts_ref[...], axis=0)
    rms = jnp.sqrt(power / (2 * F) + 1e-06)
    white = (x_ref[...].astype(F32) / rms).astype(BF16)
    own_ref[...] = white
    for k, ref in enumerate(sent):
        ref[:256, :] = white
        ref[256:, :] = lists_ref[k]


def add_list(index_ref, base, left_ref, right_ref, cross_ref, onehot_ref):
    def body(c, carry):
        rows = lax.broadcasted_iota(jnp.int32, (256, CHUNK), 0).astype(F32)
        bins = lax.broadcasted_iota(jnp.int32, (NB, CHUNK), 0).astype(F32)
        u = index_ref[pl.ds(base + c, 1), :]
        v = index_ref[pl.ds(base + CHUNKS + c, 1), :]
        b = index_ref[pl.ds(base + 2 * CHUNKS + c, 1), :]
        take_u = jnp.where(rows == u, 1.0, 0.0).astype(BF16)
        take_v = jnp.where(rows == v, 1.0, 0.0).astype(BF16)
        left = jnp.dot(left_ref[:256, :], take_u, preferred_element_type=F32)
        right = jnp.dot(right_ref[:256, :], take_v, preferred_element_type=F32)
        lr, li, rr, ri = left[:128], left[128:], right[:128], right[128:]
        lanes = pl.ds(pl.multiple_of(c * CHUNK, CHUNK), CHUNK)
        cross_ref[:128, lanes] = (lr * rr + li * ri).astype(BF16)
        cross_ref[128:, lanes] = (li * rr - lr * ri).astype(BF16)
        onehot_ref[:, lanes] = jnp.where(bins == b, 1.0, 0.0).astype(BF16)
        return carry

    lax.fori_loop(0, CHUNKS, body, 0)
    return lax.dot_general(
        onehot_ref[...], cross_ref[...], (((1,), (1,)), ((), ())), preferred_element_type=F32
    )


def pair_kernel(kind, *refs):
    if kind == "own":
        own_ref, lists_ref, out_ref, cross_ref, onehot_ref, index_ref = refs
        index_ref[:32, :] = lists_ref[...].astype(F32)
        out_ref[...] = add_list(index_ref, 0, own_ref, own_ref, cross_ref, onehot_ref)
    elif kind == "two":
        acc_ref, own_ref, lists_ref, got_ref, out_ref, cross_ref, onehot_ref, index_ref = refs
        index_ref[:32, :] = lists_ref[...].astype(F32)
        index_ref[32:, :] = got_ref[256:, :].astype(F32)
        out = acc_ref[...] + add_list(index_ref, 0, own_ref, got_ref, cross_ref, onehot_ref)
        out_ref[...] = out + add_list(index_ref, 32, got_ref, own_ref, cross_ref, onehot_ref)
    else:
        acc_ref, own_ref, lists_ref, got_ref, select_ref, out_ref, cross_ref, onehot_ref, index_ref = refs
        index_ref[:32, :] = lists_ref[...].astype(F32)
        acc = acc_ref[...] + add_list(index_ref, 0, own_ref, got_ref, cross_ref, onehot_ref)
        hi, lo = split(acc)
        pick = select_ref[...]
        owned = jnp.dot(pick, hi, preferred_element_type=F32) + jnp.dot(
            pick, lo, preferred_element_type=F32
        )
        out_ref[...] = owned.reshape(out_ref.shape)


def pair_call(kind, out_shape, *args):
    lists = 2 if kind == "two" else 1
    return pl.pallas_call(
        lambda *refs: pair_kernel(kind, *refs),
        out_shape=out_shape,
        in_specs=[VMEM] * len(args),
        out_specs=VMEM,
        scratch_shapes=[
            pltpu.VMEM((256, PAIRS), BF16),
            pltpu.VMEM((NB, PAIRS), BF16),
            pltpu.VMEM((64, CHUNK), F32),
        ],
        cost_estimate=cost(lists * 600_000_000, 1_000_000),
    )(*args)


def lag_kernel(got_ref, hi_ref, lo_ref, out_ref):
    owned = jnp.sum(got_ref[...], axis=0)
    rows = owned.shape[0]
    hi, lo = split(owned)
    both = jnp.concatenate([hi, lo], axis=0)
    for block in range(4):
        lanes = pl.ds(block * 1024, 1024)
        main = jnp.dot(both, hi_ref[:, lanes], preferred_element_type=F32)
        line = main[:rows] + main[rows:] + jnp.dot(hi, lo_ref[:, lanes], preferred_element_type=F32)
        for k in range(8):
            out_ref[block * 8 + k] = line[:, k * 128 : (k + 1) * 128].astype(out_ref.dtype)


def finish_kernel(scale, got_ref, out_ref):
    line = jnp.sum(got_ref[...].astype(F32), axis=0) * scale
    out_ref[...] = line.T


def on_device(spectra, pair_first, pair_second, pair_bin, bin_owner):
    blocks = lax.axis_size("blk")
    peers = lax.axis_size("freq")
    sensors, _, freq_dev = spectra.shape
    slots_each = 2 * NB // blocks
    scale = (F * PAIRS * blocks * blocks / NB) ** (-0.5)

    turned = jnp.transpose(spectra, (1, 2, 0)).reshape(2 * freq_dev, sensors)
    part = pl.pallas_call(
        power_kernel,
        out_shape=shape((peers, 1, sensors), F32),
        in_specs=[VMEM],
        out_specs=VMEM,
        cost_estimate=cost(200_000, 160_000),
    )(turned)
    parts = lax.all_to_all(part, "freq", 0, 0, tiled=True)

    me = lax.axis_index("freq").astype(jnp.int32).reshape(1)
    hi, lo, select = pl.pallas_call(
        factors_kernel,
        out_shape=(
            shape((2 * freq_dev, F), BF16),
            shape((2 * freq_dev, F), BF16),
            shape((2 * NB, NB), BF16),
        ),
        in_specs=[SMEM, VMEM, VMEM, pl.BlockSpec(memory_space=pl.ANY)],
        out_specs=[VMEM] * 3,
        cost_estimate=cost(10_000_000, 8_000_000),
    )(me, bin_owner.reshape(1, NB), bin_owner.reshape(NB, 1), part)

    listed = jnp.stack([pair_first[0], pair_second[0], pair_bin[0]], axis=1)
    listed = listed.reshape(blocks, 3 * CHUNKS, CHUNK).astype(BF16)
    listed = jnp.pad(listed, ((0, 0), (0, 8), (0, 0)))
    travelling = listed[blocks - 1 : blocks // 2 : -1]

    padded = 2 * freq_dev + 32
    own, *sent = pl.pallas_call(
        white_kernel,
        out_shape=[shape((2 * freq_dev, sensors), BF16)] + [shape((padded, sensors), BF16)] * 3,
        in_specs=[VMEM] * 3,
        out_specs=[VMEM] * 4,
        cost_estimate=cost(1_000_000, 800_000),
    )(parts, turned, travelling)

    def ahead(x, by):
        return lax.ppermute(x, "blk", [(i, (i + by) % blocks) for i in range(blocks)])

    got = [ahead(sent[k - 1] if k < 4 else own, k) for k in range(1, 5)]

    acc_shape = shape((NB, 2 * freq_dev), F32)
    acc = pair_call("own", acc_shape, own, listed[0])
    for k in (1, 2, 3):
        acc = pair_call("two", acc_shape, acc, own, listed[k], got[k - 1])
    stacks = pair_call(
        "last", shape((blocks, slots_each, 2 * freq_dev), F32), acc, own, listed[4], got[3], select
    )
    stacks = lax.all_to_all(stacks, "blk", 0, 0, tiled=True)

    line = pl.pallas_call(
        lag_kernel,
        out_shape=shape((peers, slots_each, freq_dev), BF16),
        in_specs=[VMEM] * 3,
        out_specs=VMEM,
        cost_estimate=cost(100_000_000, 4_500_000),
    )(stacks, hi, lo)
    line = lax.all_to_all(line, "freq", 0, 0, tiled=True)
    return pl.pallas_call(
        lambda *refs: finish_kernel(scale, *refs),
        out_shape=shape((freq_dev, slots_each), F32),
        in_specs=[VMEM],
        out_specs=VMEM,
        cost_estimate=cost(100_000, 150_000),
    )(line)


def solution(mesh):
    return jax.shard_map(
        on_device,
        mesh=mesh,
        in_specs=(
            P("blk", None, "freq"),
            P("blk", None, None),
            P("blk", None, None),
            P("blk", None, None),
            P(),
        ),
        out_specs=P("freq", "blk"),
        check_vma=False,
    )
```

```python
import functools
import math

import jax
import jax.numpy as jnp
from jax import lax
from jax.experimental import pallas as pl
from jax.experimental.pallas import tpu as pltpu
from jax.sharding import PartitionSpec as P

F = 4096
NB = 64
PAIRS = 2048
CHUNK = 256
CHUNKS = PAIRS // CHUNK
F32 = jnp.float32
BF16 = jnp.bfloat16
VMEM = pl.BlockSpec(memory_space=pltpu.VMEM)
SMEM = pl.BlockSpec(memory_space=pltpu.SMEM)


def shape(dims, dtype):
    return jax.ShapeDtypeStruct(dims, dtype)


def call(kernel, out_shape, args, mib, flops, moved, specs=None, scratch=()):
    return pl.pallas_call(
        kernel,
        out_shape=out_shape,
        in_specs=[VMEM] * len(args) if specs is None else specs,
        out_specs=jax.tree.map(lambda _: VMEM, out_shape),
        scratch_shapes=list(scratch),
        compiler_params=pltpu.CompilerParams(vmem_limit_bytes=None if mib is None else mib << 20),
        cost_estimate=pl.CostEstimate(flops=flops, bytes_accessed=moved, transcendentals=0),
    )(*args)


def split(x):
    hi = x.astype(BF16)
    return hi, (x - hi.astype(F32)).astype(BF16)


def power_kernel(x_ref, part_ref, flat_ref):
    re, im = x_ref[:, 0, :], x_ref[:, 1, :]
    flat_ref[:, :128] = re
    flat_ref[:, 128:] = im
    re, im = re.astype(F32), im.astype(F32)
    hi, lo = split(re * re + im * im)
    ones = jnp.full((8, 128), 1.0, BF16)
    dims = (((1,), (1,)), ((), ()))
    part = lax.dot_general(ones, hi, dims, preferred_element_type=F32)
    part = part + lax.dot_general(ones, lo, dims, preferred_element_type=F32)
    part_ref[...] = jnp.broadcast_to(part[None, :1], part_ref.shape)


def list_rows(lists, r):
    rows = [
        ref[0, r : r + 1, c * CHUNK : (c + 1) * CHUNK] for ref in lists for c in range(CHUNKS)
    ]
    rows = jnp.concatenate(rows, axis=0).astype(F32)
    return jnp.concatenate([rows, jnp.zeros((CHUNKS, CHUNK), F32)], axis=0)


def factors_kernel(
    me_ref, owner_ref, first_ref, second_ref, bin_ref, part_ref, out_ref, select_ref, rows_ref
):
    for r in range(rows_ref.shape[0]):
        rows_ref[r] = list_rows((first_ref, second_ref, bin_ref), r).astype(BF16)
    n = 128
    j = lax.broadcasted_iota(jnp.int32, (n, n), 0)
    i = lax.broadcasted_iota(jnp.int32, (n, n), 1)
    unit = 2.0 * math.pi / F
    first = ((i * (me_ref[0] * n + j)) & (F - 1)).astype(F32) * unit
    step = ((n * j) & (F - 1)).astype(F32) * unit
    re, im = jnp.cos(first), jnp.sin(first)
    sr, si = jnp.cos(step), jnp.sin(step)
    for block in range(F // n):
        lanes = pl.ds(block * n, n)
        out_ref[:n, lanes] = re.astype(BF16)
        out_ref[n:, lanes] = (-im).astype(BF16)
        re, im = re * sr - im * si, re * si + im * sr
    row = jnp.broadcast_to(owner_ref[...].astype(F32), (NB, NB))
    b2 = lax.broadcasted_iota(jnp.int32, (NB, NB), 0)
    b = lax.broadcasted_iota(jnp.int32, (NB, NB), 1)
    ahead = jnp.where((row.T == row) & (b2 < b), 1.0, 0.0)
    rank = jnp.sum(ahead, axis=0, keepdims=True)
    slots = select_ref.shape[0]
    slot = row[:1] * (slots // 8) + rank
    place = lax.broadcasted_iota(jnp.int32, (slots, NB), 0).astype(F32)
    select_ref[...] = jnp.where(place == slot, 1.0, 0.0).astype(BF16)


def white_kernel(parts_ref, x_ref, rows_ref, own_ref, *sent):
    power = jnp.sum(parts_ref[...], axis=0)
    rms = jnp.sqrt(power / (2 * F) + 1e-06)
    rms = jnp.broadcast_to(rms, (8, 256)).T[:, :1]
    white = (x_ref[...].astype(F32) / rms).astype(BF16)
    own_ref[...] = white
    for k, ref in enumerate(sent):
        ref[:256, :] = white
        ref[256:, :] = rows_ref[7 - k]


def column_onehot(col):
    lanes = lax.broadcasted_iota(jnp.int32, (CHUNK, 256), 1).astype(F32).astype(BF16)
    same = lanes == jnp.broadcast_to(col, (CHUNK, 256))
    return jnp.where(same, jnp.asarray(1.0, BF16), jnp.asarray(0.0, BF16))


def add_list(rows, left_block, right_block):
    index = rows[: 2 * CHUNKS].T.astype(BF16)
    take_u = [column_onehot(index[:, c : c + 1]) for c in range(CHUNKS)]
    take_v = [column_onehot(index[:, CHUNKS + c : CHUNKS + c + 1]) for c in range(CHUNKS)]
    left = jnp.dot(jnp.concatenate(take_u, 0), left_block, preferred_element_type=F32)
    right = jnp.dot(jnp.concatenate(take_v, 0), right_block, preferred_element_type=F32)
    lr, li, rr, ri = left[:, :128], left[:, 128:], right[:, :128], right[:, 128:]
    re = (lr * rr + li * ri).astype(BF16)
    im = (li * rr - lr * ri).astype(BF16)
    cross = jnp.concatenate([re, im], axis=1)
    bins = lax.broadcasted_iota(jnp.int32, (NB, CHUNK), 0).astype(F32)
    onehot = [
        jnp.where(bins == rows[2 * CHUNKS + c : 2 * CHUNKS + c + 1], 1.0, 0.0).astype(BF16)
        for c in range(CHUNKS)
    ]
    return jnp.dot(jnp.concatenate(onehot, 1), cross, preferred_element_type=F32)


def pair_kernel(steps, first, last, *refs):
    refs = list(refs)
    acc = None if first else refs.pop(0)[...]
    own_ref, rows_ref = refs[:2]
    got = refs[2 : 2 + len(steps)]
    out_ref = refs[-1]
    if first:
        acc = add_list(rows_ref[0].astype(F32), own_ref[...], own_ref[...])
    for k, got_ref in zip(steps, got):
        acc = acc + add_list(rows_ref[k].astype(F32), own_ref[...], got_ref[:256, :])
        if k < 4:
            acc = acc + add_list(got_ref[256:, :].astype(F32), got_ref[:256, :], own_ref[...])
    if last:
        pick = refs[2 + len(steps)][...]
        owned = jnp.dot(pick, acc.astype(BF16), preferred_element_type=F32)
        acc = owned.reshape(out_ref.shape)
    out_ref[...] = acc.astype(out_ref.dtype)


def pair_call(steps, out_shape, acc, own, lists, got, select):
    first, last = acc is None, select is not None
    args = [] if first else [acc]
    args += [own, lists, *got]
    args += [select] if last else []
    kernel = functools.partial(pair_kernel, steps, first, last)
    return call(kernel, out_shape, args, 20, 1_200_000_000 * max(len(steps), 1), 1_000_000)


def lag_kernel(got_ref, factors_ref, out_ref):
    owned = jnp.sum(got_ref[...].astype(F32), axis=0)
    rows = owned.shape[0]
    both = jnp.concatenate(split(owned), axis=0)
    for block in range(4):
        lanes = pl.ds(block * 1024, 1024)
        line = jnp.dot(both, factors_ref[:, lanes], preferred_element_type=F32)
        line = line[:rows] + line[rows:]
        for k in range(8):
            out_ref[block * 8 + k] = line[:, k * 128 : (k + 1) * 128].astype(out_ref.dtype)


def finish_kernel(scale, got_ref, out_ref):
    out_ref[...] = jnp.sum(got_ref[...].astype(F32), axis=0) * scale


def on_device(spectra, pair_first, pair_second, pair_bin, bin_owner):
    blocks = lax.axis_size("blk")
    peers = lax.axis_size("freq")
    sensors, _, freq_dev = spectra.shape
    width = 2 * freq_dev
    slots_each = 2 * NB // blocks
    scale = (F * PAIRS * blocks * blocks / NB) ** (-0.5)
    lists = (pair_first, pair_second, pair_bin)

    part, flat = call(
        power_kernel,
        [shape((peers, 1, sensors), F32), shape((sensors, width), BF16)],
        (spectra,), None, 1_000_000, 300_000,
    )
    parts = lax.all_to_all(part, "freq", 0, 0, tiled=True)

    me = lax.axis_index("freq").astype(jnp.int32).reshape(1)
    factors, select, rows = call(
        factors_kernel,
        [
            shape((width, F), BF16),
            shape((2 * NB, NB), BF16),
            shape((blocks, 4 * CHUNKS, CHUNK), BF16),
        ],
        (me, bin_owner.reshape(1, NB), *lists, part), 8, 10_000_000, 8_000_000,
        specs=[SMEM] + [VMEM] * 4 + [pl.BlockSpec(memory_space=pl.ANY)],
    )

    own, *sent = call(
        white_kernel,
        [shape((sensors, width), BF16)] + [shape((sensors + 32, width), BF16)] * 3,
        (parts, flat, rows), 4, 1_000_000, 800_000,
    )

    def ahead(x, by):
        return lax.ppermute(x, "blk", [(i, (i + by) % blocks) for i in range(blocks)])

    got = {k: ahead(sent[k - 1] if k < 4 else own, k) for k in (2, 1, 3, 4)}

    acc_shape = shape((NB, width), F32)
    acc = pair_call((), acc_shape, None, own, rows, (), None)
    acc = pair_call((1, 3), acc_shape, acc, own, rows, (got[1], got[3]), None)
    stacks = pair_call(
        (2, 4), shape((blocks, slots_each, width), BF16), acc, own, rows, (got[2], got[4]), select
    )
    stacks = lax.all_to_all(stacks, "blk", 0, 0, tiled=True)

    line = call(
        lag_kernel, shape((peers, slots_each, freq_dev), BF16), (stacks, factors), 6, 100_000_000, 2_500_000
    )
    line = lax.all_to_all(line, "freq", 0, 0, tiled=True)
    out = call(
        functools.partial(finish_kernel, scale), shape((slots_each, freq_dev), F32), (line,), 2, 100_000, 150_000
    )
    return out.T


def solution(mesh):
    return jax.shard_map(
        on_device,
        mesh=mesh,
        in_specs=(
            P("blk", None, "freq"),
            P("blk", None, None),
            P("blk", None, None),
            P("blk", None, None),
            P(),
        ),
        out_specs=P("freq", "blk"),
        check_vma=False,
    )
```

```python
import functools
import math

import jax
import jax.numpy as jnp
from jax import lax
from jax.experimental import pallas as pl
from jax.experimental.pallas import tpu as pltpu
from jax.sharding import PartitionSpec as P


F = 4096
NB = 64
PAIRS = 2048
CHUNK = 256
CHUNKS = PAIRS // CHUNK
F32 = jnp.float32
BF16 = jnp.bfloat16
VMEM = pl.BlockSpec(memory_space=pltpu.VMEM)
SMEM = pl.BlockSpec(memory_space=pltpu.SMEM)


def shape(dims, dtype):
    return jax.ShapeDtypeStruct(dims, dtype)


def call(kernel, out_shape, args, mib, flops, moved, specs=None, scratch=()):
    return pl.pallas_call(
        kernel,
        out_shape=out_shape,
        in_specs=[VMEM] * len(args) if specs is None else specs,
        out_specs=jax.tree.map(lambda _: VMEM, out_shape),
        scratch_shapes=list(scratch),
        compiler_params=pltpu.CompilerParams(vmem_limit_bytes=None if mib is None else mib << 20),
        cost_estimate=pl.CostEstimate(flops=flops, bytes_accessed=moved, transcendentals=0),
    )(*args)


def split(x):
    hi = x.astype(BF16)
    return hi, (x - hi.astype(F32)).astype(BF16)


def power_kernel(x_ref, part_ref, flat_ref, wide_ref):
    wide_ref[...] = x_ref[...].astype(F32)
    re = wide_ref[pl.ds(0, 256, stride=2), :]
    im = wide_ref[pl.ds(1, 256, stride=2), :]
    flat_ref[:, :128] = re.astype(BF16)
    flat_ref[:, 128:] = im.astype(BF16)
    hi, lo = split(re * re + im * im)
    ones = jnp.full((8, 128), 1.0, BF16)
    dims = (((1,), (1,)), ((), ()))
    part = lax.dot_general(ones, hi, dims, preferred_element_type=F32)
    part = part + lax.dot_general(ones, lo, dims, preferred_element_type=F32)
    part_ref[...] = jnp.broadcast_to(part[None, :1], part_ref.shape)


def list_rows(lists, r):
    rows = [
        ref[0, r : r + 1, c * CHUNK : (c + 1) * CHUNK] for ref in lists for c in range(CHUNKS)
    ]
    rows = jnp.concatenate(rows, axis=0).astype(F32)
    return jnp.concatenate([rows, jnp.zeros((CHUNKS, CHUNK), F32)], axis=0)


def rows_kernel(first_ref, second_ref, bin_ref, part_ref, rows_ref):
    for r in range(rows_ref.shape[0]):
        rows_ref[r] = list_rows((first_ref, second_ref, bin_ref), r).astype(BF16)


def factors_kernel(me_ref, owner_ref, after_ref, out_ref, select_ref):
    n = 128
    j = lax.broadcasted_iota(jnp.int32, (n, n), 0)
    i = lax.broadcasted_iota(jnp.int32, (n, n), 1)
    unit = 2.0 * math.pi / F
    first = ((i * (me_ref[0] * n + j)) & (F - 1)).astype(F32) * unit
    step = ((n * j) & (F - 1)).astype(F32) * unit
    re, im = jnp.cos(first), jnp.sin(first)
    sr, si = jnp.cos(step), jnp.sin(step)
    for block in range(F // n):
        lanes = pl.ds(block * n, n)
        out_ref[:n, lanes] = re.astype(BF16)
        out_ref[n:, lanes] = (-im).astype(BF16)
        re, im = re * sr - im * si, re * si + im * sr
    row = jnp.broadcast_to(owner_ref[...].astype(F32), (NB, NB))
    b2 = lax.broadcasted_iota(jnp.int32, (NB, NB), 0)
    b = lax.broadcasted_iota(jnp.int32, (NB, NB), 1)
    ahead = jnp.where((row.T == row) & (b2 < b), 1.0, 0.0)
    rank = jnp.sum(ahead, axis=0, keepdims=True)
    slots = select_ref.shape[0]
    slot = row[:1] * (slots // 8) + rank
    place = lax.broadcasted_iota(jnp.int32, (slots, NB), 0).astype(F32)
    select_ref[...] = jnp.where(place == slot, 1.0, 0.0).astype(BF16)


def white_kernel(parts_ref, x_ref, rows_ref, own_ref, *sent):
    power = jnp.sum(parts_ref[...], axis=0)
    rms = jnp.sqrt(power / (2 * F) + 1e-06)
    rms = jnp.broadcast_to(rms, (8, 256)).T[:, :1]
    white = (x_ref[...].astype(F32) / rms).astype(BF16)
    own_ref[...] = white
    for k, ref in enumerate(sent):
        ref[:256, :] = white
        ref[256:, :] = rows_ref[7 - k]


def column_onehot(col):
    lanes = lax.broadcasted_iota(jnp.int32, (CHUNK, 256), 1).astype(F32).astype(BF16)
    same = lanes == jnp.broadcast_to(col, (CHUNK, 256))
    return jnp.where(same, jnp.asarray(1.0, BF16), jnp.asarray(0.0, BF16))


def add_list(rows, left_block, right_block):
    index = rows[: 2 * CHUNKS].T.astype(BF16)
    take_u = [column_onehot(index[:, c : c + 1]) for c in range(CHUNKS)]
    take_v = [column_onehot(index[:, CHUNKS + c : CHUNKS + c + 1]) for c in range(CHUNKS)]
    left = jnp.dot(jnp.concatenate(take_u, 0), left_block, preferred_element_type=F32)
    right = jnp.dot(jnp.concatenate(take_v, 0), right_block, preferred_element_type=F32)
    lr, li, rr, ri = left[:, :128], left[:, 128:], right[:, :128], right[:, 128:]
    re = (lr * rr + li * ri).astype(BF16)
    im = (li * rr - lr * ri).astype(BF16)
    cross = jnp.concatenate([re, im], axis=1)
    bins = lax.broadcasted_iota(jnp.int32, (NB, CHUNK), 0).astype(F32)
    onehot = [
        jnp.where(bins == rows[2 * CHUNKS + c : 2 * CHUNKS + c + 1], 1.0, 0.0).astype(BF16)
        for c in range(CHUNKS)
    ]
    return jnp.dot(jnp.concatenate(onehot, 1), cross, preferred_element_type=F32)


def pair_kernel(steps, first, last, *refs):
    refs = list(refs)
    acc = None if first else refs.pop(0)[...]
    own_ref, rows_ref = refs[:2]
    got = refs[2 : 2 + len(steps)]
    out_ref = refs[-1]
    if first:
        acc = add_list(rows_ref[0].astype(F32), own_ref[...], own_ref[...])
    for k, got_ref in zip(steps, got):
        acc = acc + add_list(rows_ref[k].astype(F32), own_ref[...], got_ref[:256, :])
        if k < 4:
            acc = acc + add_list(got_ref[256:, :].astype(F32), got_ref[:256, :], own_ref[...])
    if last:
        pick = refs[2 + len(steps)][...]
        owned = jnp.dot(pick, acc.astype(BF16), preferred_element_type=F32)
        acc = owned.reshape(out_ref.shape)
    out_ref[...] = acc.astype(out_ref.dtype)


def pair_call(steps, out_shape, acc, own, lists, got, select):
    first, last = acc is None, select is not None
    args = [] if first else [acc]
    args += [own, lists, *got]
    args += [select] if last else []
    kernel = functools.partial(pair_kernel, steps, first, last)
    return call(kernel, out_shape, args, 20, 1_200_000_000 * max(len(steps), 1), 1_000_000)


def lag_kernel(got_ref, factors_ref, out_ref):
    owned = jnp.sum(got_ref[...].astype(F32), axis=0)
    rows = owned.shape[0]
    both = jnp.concatenate(split(owned), axis=0)
    for block in range(4):
        lanes = pl.ds(block * 1024, 1024)
        line = jnp.dot(both, factors_ref[:, lanes], preferred_element_type=F32)
        line = line[:rows] + line[rows:]
        for k in range(8):
            out_ref[block * 8 + k] = line[:, k * 128 : (k + 1) * 128].astype(out_ref.dtype)


def finish_kernel(scale, got_ref, out_ref):
    out_ref[...] = jnp.sum(got_ref[...].astype(F32), axis=0) * scale


def on_device(spectra, pair_first, pair_second, pair_bin, bin_owner):
    blocks = lax.axis_size("blk")
    peers = lax.axis_size("freq")
    sensors, _, freq_dev = spectra.shape
    width = 2 * freq_dev
    slots_each = 2 * NB // blocks
    scale = (F * PAIRS * blocks * blocks / NB) ** (-0.5)
    lists = (pair_first, pair_second, pair_bin)

    part, flat = call(
        power_kernel,
        [shape((peers, 1, sensors), F32), shape((sensors, width), BF16)],
        (spectra.reshape(2 * sensors, freq_dev),), 4, 1_000_000, 300_000,
        scratch=[pltpu.VMEM((2 * sensors, freq_dev), F32)],
    )
    parts = lax.all_to_all(part, "freq", 0, 0, tiled=True)

    anywhere = pl.BlockSpec(memory_space=pl.ANY)
    rows = call(
        rows_kernel, shape((blocks, 4 * CHUNKS, CHUNK), BF16), (*lists, part), 4, 1_000_000, 400_000,
        specs=[VMEM] * 3 + [anywhere],
    )

    own, *sent = call(
        white_kernel,
        [shape((sensors, width), BF16)] + [shape((sensors + 32, width), BF16)] * 3,
        (parts, flat, rows), 4, 1_000_000, 800_000,
    )

    def ahead(x, by):
        return lax.ppermute(x, "blk", [(i, (i + by) % blocks) for i in range(blocks)])

    got = {k: ahead(sent[k - 1] if k < 4 else own, k) for k in (2, 4, 1, 3)}

    acc_shape = shape((NB, width), F32)
    acc = pair_call((), acc_shape, None, own, rows, (), None)
    for k in (4, 1, 3):
        acc = pair_call((k,), acc_shape, acc, own, rows, (got[k],), None)
    me = lax.axis_index("freq").astype(jnp.int32).reshape(1)
    factors, select = call(
        factors_kernel, [shape((width, F), BF16), shape((2 * NB, NB), BF16)],
        (me, bin_owner.reshape(1, NB), acc), 8, 10_000_000, 8_000_000,
        specs=[SMEM, VMEM, anywhere],
    )
    stacks_shape = shape((blocks, slots_each, width), BF16)
    stacks = pair_call((2,), stacks_shape, acc, own, rows, (got[2],), select)
    stacks = lax.all_to_all(stacks, "blk", 0, 0, tiled=True)

    line = call(
        lag_kernel, shape((peers, slots_each, freq_dev), BF16), (stacks, factors), 6, 100_000_000, 2_500_000
    )
    line = lax.all_to_all(line, "freq", 0, 0, tiled=True)
    out = call(
        functools.partial(finish_kernel, scale), shape((slots_each, freq_dev), F32), (line,), 2, 100_000, 150_000
    )
    return out.T


def solution(mesh):
    return jax.shard_map(
        on_device,
        mesh=mesh,
        in_specs=(
            P("blk", None, "freq"),
            P("blk", None, None),
            P("blk", None, None),
            P("blk", None, None),
            P(),
        ),
        out_specs=P("freq", "blk"),
        check_vma=False,
    )
```

```python
import functools
import math

import jax
import jax.numpy as jnp
from jax import lax
from jax.experimental import pallas as pl
from jax.experimental.pallas import tpu as pltpu
from jax.sharding import PartitionSpec as P


F = 4096
NB = 64
PAIRS = 2048
CHUNK = 256
CHUNKS = PAIRS // CHUNK
F32 = jnp.float32
BF16 = jnp.bfloat16
VMEM = pl.BlockSpec(memory_space=pltpu.VMEM)
SMEM = pl.BlockSpec(memory_space=pltpu.SMEM)


def target(kind, a):
    if kind == "beside":
        return a - a % 4 + (a + 1) % 4
    if kind == "corner":
        return (a - a % 4 + 4) % 8 + (a + 3) % 4
    if kind == "across":
        return (a + 4) % 8
    return (a + 2) % 8


def source(kind, a):
    if kind == "beside":
        return a - a % 4 + (a + 3) % 4
    if kind == "corner":
        return (a - a % 4 + 4) % 8 + (a + 1) % 4
    if kind == "across":
        return (a + 4) % 8
    return (a + 6) % 8


TWO_WAY = ("beside", "corner", "far")


def shape(dims, dtype):
    return jax.ShapeDtypeStruct(dims, dtype)


def call(kernel, out_shape, args, mib, flops, moved, specs=None, scratch=()):
    return pl.pallas_call(
        kernel,
        out_shape=out_shape,
        in_specs=[VMEM] * len(args) if specs is None else specs,
        out_specs=jax.tree.map(lambda _: VMEM, out_shape),
        scratch_shapes=list(scratch),
        compiler_params=pltpu.CompilerParams(vmem_limit_bytes=None if mib is None else mib << 20),
        cost_estimate=pl.CostEstimate(flops=flops, bytes_accessed=moved, transcendentals=0),
    )(*args)


def split(x):
    hi = x.astype(BF16)
    return hi, (x - hi.astype(F32)).astype(BF16)


def power_kernel(x_ref, part_ref, flat_ref, wide_ref):
    wide_ref[...] = x_ref[...].astype(F32)
    re = wide_ref[pl.ds(0, 256, stride=2), :]
    im = wide_ref[pl.ds(1, 256, stride=2), :]
    flat_ref[:, :128] = re.astype(BF16)
    flat_ref[:, 128:] = im.astype(BF16)
    hi, lo = split(re * re + im * im)
    ones = jnp.full((8, 128), 1.0, BF16)
    dims = (((1,), (1,)), ((), ()))
    part = lax.dot_general(ones, hi, dims, preferred_element_type=F32)
    part = part + lax.dot_general(ones, lo, dims, preferred_element_type=F32)
    part_ref[...] = jnp.broadcast_to(part[None, :1], part_ref.shape)


def list_rows(lists, r):
    rows = [
        ref[0, r : r + 1, c * CHUNK : (c + 1) * CHUNK] for ref in lists for c in range(CHUNKS)
    ]
    rows = jnp.concatenate(rows, axis=0).astype(F32)
    return jnp.concatenate([rows, jnp.zeros((CHUNKS, CHUNK), F32)], axis=0)


def factors_kernel(me_ref, first_ref, second_ref, bin_ref, part_ref, out_ref, rows_ref):
    for r in range(rows_ref.shape[0]):
        rows_ref[r] = list_rows((first_ref, second_ref, bin_ref), r).astype(BF16)
    n = 128
    j = lax.broadcasted_iota(jnp.int32, (n, n), 0)
    i = lax.broadcasted_iota(jnp.int32, (n, n), 1)
    unit = 2.0 * math.pi / F
    first = ((i * (me_ref[0] * n + j)) & (F - 1)).astype(F32) * unit
    step = ((n * j) & (F - 1)).astype(F32) * unit
    re, im = jnp.cos(first), jnp.sin(first)
    sr, si = jnp.cos(step), jnp.sin(step)
    for block in range(F // n):
        lanes = pl.ds(block * n, n)
        out_ref[:n, lanes] = re.astype(BF16)
        out_ref[n:, lanes] = (-im).astype(BF16)
        re, im = re * sr - im * si, re * si + im * sr


def select_kernel(owner_ref, after_ref, select_ref):
    row = jnp.broadcast_to(owner_ref[...].astype(F32), (NB, NB))
    b2 = lax.broadcasted_iota(jnp.int32, (NB, NB), 0)
    b = lax.broadcasted_iota(jnp.int32, (NB, NB), 1)
    ahead = jnp.where((row.T == row) & (b2 < b), 1.0, 0.0)
    rank = jnp.sum(ahead, axis=0, keepdims=True)
    slots = select_ref.shape[0]
    slot = row[:1] * (slots // 8) + rank
    place = lax.broadcasted_iota(jnp.int32, (slots, NB), 0).astype(F32)
    select_ref[...] = jnp.where(place == slot, 1.0, 0.0).astype(BF16)


def white_kernel(parts_ref, x_ref, rows_ref, own_ref, *sent):
    power = jnp.sum(parts_ref[...], axis=0)
    rms = jnp.sqrt(power / (2 * F) + 1e-06)
    rms = jnp.broadcast_to(rms, (8, 256)).T[:, :1]
    white = (x_ref[...].astype(F32) / rms).astype(BF16)
    own_ref[...] = white
    me = lax.axis_index("blk")
    for kind, ref in zip(TWO_WAY, sent):
        ref[:256, :] = white
        ref[256:, :] = rows_ref[lax.rem(me - target(kind, me) + 8, 8)]


def column_onehot(col):
    lanes = lax.broadcasted_iota(jnp.int32, (CHUNK, 256), 1).astype(F32).astype(BF16)
    same = lanes == jnp.broadcast_to(col, (CHUNK, 256))
    return jnp.where(same, jnp.asarray(1.0, BF16), jnp.asarray(0.0, BF16))


def add_list(rows, left_block, right_block):
    index = rows[: 2 * CHUNKS].T.astype(BF16)
    take_u = [column_onehot(index[:, c : c + 1]) for c in range(CHUNKS)]
    take_v = [column_onehot(index[:, CHUNKS + c : CHUNKS + c + 1]) for c in range(CHUNKS)]
    left = jnp.dot(jnp.concatenate(take_u, 0), left_block, preferred_element_type=F32)
    right = jnp.dot(jnp.concatenate(take_v, 0), right_block, preferred_element_type=F32)
    lr, li, rr, ri = left[:, :128], left[:, 128:], right[:, :128], right[:, 128:]
    re = (lr * rr + li * ri).astype(BF16)
    im = (li * rr - lr * ri).astype(BF16)
    cross = jnp.concatenate([re, im], axis=1)
    bins = lax.broadcasted_iota(jnp.int32, (NB, CHUNK), 0).astype(F32)
    onehot = [
        jnp.where(bins == rows[2 * CHUNKS + c : 2 * CHUNKS + c + 1], 1.0, 0.0).astype(BF16)
        for c in range(CHUNKS)
    ]
    return jnp.dot(jnp.concatenate(onehot, 1), cross, preferred_element_type=F32)


def pair_kernel(kinds, first, last, *refs):
    refs = list(refs)
    acc = None if first else refs.pop(0)[...]
    own_ref, rows_ref = refs[:2]
    got = refs[2 : 2 + len(kinds)]
    out_ref = refs[-1]
    if first:
        acc = add_list(rows_ref[0].astype(F32), own_ref[...], own_ref[...])
    me = lax.axis_index("blk")
    for kind, got_ref in zip(kinds, got):
        mine = rows_ref[lax.rem(me - source(kind, me) + 8, 8)].astype(F32)
        acc = acc + add_list(mine, own_ref[...], got_ref[:256, :])
        if kind in TWO_WAY:
            acc = acc + add_list(got_ref[256:, :].astype(F32), got_ref[:256, :], own_ref[...])
    if last:
        pick = refs[2 + len(kinds)][...]
        owned = jnp.dot(pick, acc.astype(BF16), preferred_element_type=F32)
        acc = owned.reshape(out_ref.shape)
    out_ref[...] = acc.astype(out_ref.dtype)


def pair_call(kinds, out_shape, acc, own, lists, got, select):
    first, last = acc is None, select is not None
    args = [] if first else [acc]
    args += [own, lists, *got]
    args += [select] if last else []
    kernel = functools.partial(pair_kernel, kinds, first, last)
    return call(kernel, out_shape, args, 20, 1_200_000_000 * max(len(kinds), 1), 1_000_000)


def lag_kernel(got_ref, factors_ref, out_ref):
    owned = jnp.sum(got_ref[...].astype(F32), axis=0)
    rows = owned.shape[0]
    both = jnp.concatenate(split(owned), axis=0)
    for block in range(4):
        lanes = pl.ds(block * 1024, 1024)
        line = jnp.dot(both, factors_ref[:, lanes], preferred_element_type=F32)
        line = line[:rows] + line[rows:]
        for k in range(8):
            out_ref[block * 8 + k] = line[:, k * 128 : (k + 1) * 128].astype(out_ref.dtype)


def finish_kernel(scale, got_ref, out_ref):
    out_ref[...] = jnp.sum(got_ref[...].astype(F32), axis=0) * scale


def on_device(spectra, pair_first, pair_second, pair_bin, bin_owner):
    blocks = lax.axis_size("blk")
    peers = lax.axis_size("freq")
    sensors, _, freq_dev = spectra.shape
    width = 2 * freq_dev
    slots_each = 2 * NB // blocks
    scale = (F * PAIRS * blocks * blocks / NB) ** (-0.5)
    lists = (pair_first, pair_second, pair_bin)

    part, flat = call(
        power_kernel,
        [shape((peers, 1, sensors), F32), shape((sensors, width), BF16)],
        (spectra.reshape(2 * sensors, freq_dev),), 4, 1_000_000, 300_000,
        scratch=[pltpu.VMEM((2 * sensors, freq_dev), F32)],
    )
    parts = lax.all_to_all(part, "freq", 0, 0, tiled=True)

    anywhere = pl.BlockSpec(memory_space=pl.ANY)
    me = lax.axis_index("freq").astype(jnp.int32).reshape(1)
    factors, rows = call(
        factors_kernel,
        [shape((width, F), BF16), shape((blocks, 4 * CHUNKS, CHUNK), BF16)],
        (me, *lists, part), 8, 10_000_000, 8_000_000,
        specs=[SMEM] + [VMEM] * 3 + [anywhere],
    )

    own, *sent = call(
        white_kernel,
        [shape((sensors, width), BF16)] + [shape((sensors + 32, width), BF16)] * 3,
        (parts, flat, rows), 4, 1_000_000, 800_000,
    )

    sent = dict(zip(TWO_WAY, sent), across=own)

    def exchange(kind):
        return lax.ppermute(sent[kind], "blk", [(a, target(kind, a)) for a in range(blocks)])

    got = {kind: exchange(kind) for kind in ("far", "beside", "corner", "across")}

    acc_shape = shape((NB, width), F32)
    acc = pair_call((), acc_shape, None, own, rows, (), None)
    for kind in ("beside", "across", "corner"):
        acc = pair_call((kind,), acc_shape, acc, own, rows, (got[kind],), None)
    select = call(
        select_kernel, shape((2 * NB, NB), BF16), (bin_owner.reshape(1, NB), acc), 2, 100_000, 30_000,
        specs=[VMEM, anywhere],
    )
    stacks_shape = shape((blocks, slots_each, width), BF16)
    stacks = pair_call(("far",), stacks_shape, acc, own, rows, (got["far"],), select)
    stacks = lax.all_to_all(stacks, "blk", 0, 0, tiled=True)

    line = call(
        lag_kernel, shape((peers, slots_each, freq_dev), BF16), (stacks, factors), 6, 100_000_000, 2_500_000
    )
    line = lax.all_to_all(line, "freq", 0, 0, tiled=True)
    out = call(
        functools.partial(finish_kernel, scale), shape((slots_each, freq_dev), F32), (line,), 2, 100_000, 150_000
    )
    return out.T


def solution(mesh):
    return jax.shard_map(
        on_device,
        mesh=mesh,
        in_specs=(
            P("blk", None, "freq"),
            P("blk", None, None),
            P("blk", None, None),
            P("blk", None, None),
            P(),
        ),
        out_specs=P("freq", "blk"),
        check_vma=False,
    )
```

```python
import functools
import math

import jax
import jax.numpy as jnp
from jax import lax
from jax.experimental import pallas as pl
from jax.experimental.pallas import tpu as pltpu
from jax.sharding import PartitionSpec as P


F = 4096
NB = 64
PAIRS = 2048
CHUNK = 256
CHUNKS = PAIRS // CHUNK
F32 = jnp.float32
BF16 = jnp.bfloat16
VMEM = pl.BlockSpec(memory_space=pltpu.VMEM)
SMEM = pl.BlockSpec(memory_space=pltpu.SMEM)


STEPS = {"beside": (0, 3), "across": (1, 0), "two": (0, 2)}
CARRIED = {"beside": ("own", "across"), "across": ("beside", "two"), "two": ()}


def place(kind, a):
    dx, dy = STEPS.get(kind, (0, 0))
    return (a - a % 4 + 4 * dx) % 8 + (a + dy) % 4


def reader(kind, a):
    dx, dy = STEPS[kind]
    return (a - a % 4 + 4 * dx) % 8 + (a + 4 - dy) % 4


def shape(dims, dtype):
    return jax.ShapeDtypeStruct(dims, dtype)


def call(kernel, out_shape, args, mib, flops, moved, specs=None, scratch=()):
    return pl.pallas_call(
        kernel,
        out_shape=out_shape,
        in_specs=[VMEM] * len(args) if specs is None else specs,
        out_specs=jax.tree.map(lambda _: VMEM, out_shape),
        scratch_shapes=list(scratch),
        compiler_params=pltpu.CompilerParams(vmem_limit_bytes=None if mib is None else mib << 20),
        cost_estimate=pl.CostEstimate(flops=flops, bytes_accessed=moved, transcendentals=0),
    )(*args)


def split(x):
    hi = x.astype(BF16)
    return hi, (x - hi.astype(F32)).astype(BF16)


def power_kernel(x_ref, part_ref, flat_ref, wide_ref):
    wide_ref[...] = x_ref[...].astype(F32)
    re = wide_ref[pl.ds(0, 256, stride=2), :]
    im = wide_ref[pl.ds(1, 256, stride=2), :]
    flat_ref[:, :128] = re.astype(BF16)
    flat_ref[:, 128:] = im.astype(BF16)
    hi, lo = split(re * re + im * im)
    ones = jnp.full((8, 128), 1.0, BF16)
    dims = (((1,), (1,)), ((), ()))
    part = lax.dot_general(ones, hi, dims, preferred_element_type=F32)
    part = part + lax.dot_general(ones, lo, dims, preferred_element_type=F32)
    part_ref[...] = jnp.broadcast_to(part[None, :1], part_ref.shape)


def list_rows(lists, r):
    rows = [
        ref[0, r : r + 1, c * CHUNK : (c + 1) * CHUNK] for ref in lists for c in range(CHUNKS)
    ]
    rows = jnp.concatenate(rows, axis=0).astype(F32)
    return jnp.concatenate([rows, jnp.zeros((CHUNKS, CHUNK), F32)], axis=0)


def factors_kernel(me_ref, first_ref, second_ref, bin_ref, part_ref, out_ref, rows_ref):
    for r in range(rows_ref.shape[0]):
        rows_ref[r] = list_rows((first_ref, second_ref, bin_ref), r).astype(BF16)
    n = 128
    j = lax.broadcasted_iota(jnp.int32, (n, n), 0)
    i = lax.broadcasted_iota(jnp.int32, (n, n), 1)
    unit = 2.0 * math.pi / F
    first = ((i * (me_ref[0] * n + j)) & (F - 1)).astype(F32) * unit
    step = ((n * j) & (F - 1)).astype(F32) * unit
    re, im = jnp.cos(first), jnp.sin(first)
    sr, si = jnp.cos(step), jnp.sin(step)
    for block in range(F // n):
        lanes = pl.ds(block * n, n)
        out_ref[:n, lanes] = re.astype(BF16)
        out_ref[n:, lanes] = (-im).astype(BF16)
        re, im = re * sr - im * si, re * si + im * sr


def select_kernel(owner_ref, after_ref, select_ref):
    row = jnp.broadcast_to(owner_ref[...].astype(F32), (NB, NB))
    b2 = lax.broadcasted_iota(jnp.int32, (NB, NB), 0)
    b = lax.broadcasted_iota(jnp.int32, (NB, NB), 1)
    ahead = jnp.where((row.T == row) & (b2 < b), 1.0, 0.0)
    rank = jnp.sum(ahead, axis=0, keepdims=True)
    slots = select_ref.shape[0]
    slot = row[:1] * (slots // 8) + rank
    place = lax.broadcasted_iota(jnp.int32, (slots, NB), 0).astype(F32)
    select_ref[...] = jnp.where(place == slot, 1.0, 0.0).astype(BF16)


def white_kernel(parts_ref, x_ref, rows_ref, own_ref, *sent):
    power = jnp.sum(parts_ref[...], axis=0)
    rms = jnp.sqrt(power / (2 * F) + 1e-06)
    rms = jnp.broadcast_to(rms, (8, 256)).T[:, :1]
    white = (x_ref[...].astype(F32) / rms).astype(BF16)
    own_ref[...] = white
    me = lax.axis_index("blk")
    for kind, ref in zip(STEPS, sent):
        ref[:256, :] = white
        for k, other in enumerate(CARRIED[kind]):
            partner = place(other, reader(kind, me))
            first = 256 + 3 * CHUNKS * k
            ref[first : first + 3 * CHUNKS, :] = rows_ref[(me - partner + 8) % 8, : 3 * CHUNKS]


def column_onehot(col):
    lanes = lax.broadcasted_iota(jnp.int32, (CHUNK, 256), 1).astype(F32).astype(BF16)
    same = lanes == jnp.broadcast_to(col, (CHUNK, 256))
    return jnp.where(same, jnp.asarray(1.0, BF16), jnp.asarray(0.0, BF16))


def add_list(rows, left_block, right_block):
    index = rows[: 2 * CHUNKS].T.astype(BF16)
    take_u = [column_onehot(index[:, c : c + 1]) for c in range(CHUNKS)]
    take_v = [column_onehot(index[:, CHUNKS + c : CHUNKS + c + 1]) for c in range(CHUNKS)]
    left = jnp.dot(jnp.concatenate(take_u, 0), left_block, preferred_element_type=F32)
    right = jnp.dot(jnp.concatenate(take_v, 0), right_block, preferred_element_type=F32)
    lr, li, rr, ri = left[:, :128], left[:, 128:], right[:, :128], right[:, 128:]
    re = (lr * rr + li * ri).astype(BF16)
    im = (li * rr - lr * ri).astype(BF16)
    cross = jnp.concatenate([re, im], axis=1)
    bins = lax.broadcasted_iota(jnp.int32, (NB, CHUNK), 0).astype(F32)
    onehot = [
        jnp.where(bins == rows[2 * CHUNKS + c : 2 * CHUNKS + c + 1], 1.0, 0.0).astype(BF16)
        for c in range(CHUNKS)
    ]
    return jnp.dot(jnp.concatenate(onehot, 1), cross, preferred_element_type=F32)


def pair_kernel(jobs, kinds, first, last, *refs):
    refs = list(refs)
    acc = None if first else refs.pop(0)[...]
    rows_ref = refs.pop(0)
    held = dict(zip(kinds, refs))
    out_ref = refs[-1]
    me = lax.axis_index("blk")
    for one, other in jobs:
        if one == "own":
            rows = rows_ref[(me - place(other, me) + 8) % 8].astype(F32)
        else:
            start = 256 + 3 * CHUNKS * CARRIED[one].index(other)
            rows = held[one][start : start + 3 * CHUNKS, :].astype(F32)
        part = add_list(rows, held[one][:256, :], held[other][:256, :])
        acc = part if acc is None else acc + part
    if last:
        owned = jnp.dot(refs[-2][...], acc.astype(BF16), preferred_element_type=F32)
        acc = owned.reshape(out_ref.shape)
    out_ref[...] = acc.astype(out_ref.dtype)


def pair_call(jobs, out_shape, acc, rows, held, select):
    first, last = acc is None, select is not None
    kinds = tuple(dict.fromkeys(kind for job in jobs for kind in job))
    args = [] if first else [acc]
    args += [rows, *(held[kind] for kind in kinds)]
    args += [select] if last else []
    kernel = functools.partial(pair_kernel, jobs, kinds, first, last)
    return call(kernel, out_shape, args, 20, 600_000_000 * len(jobs), 1_000_000)


def lag_kernel(got_ref, factors_ref, out_ref):
    owned = jnp.sum(got_ref[...].astype(F32), axis=0)
    rows = owned.shape[0]
    both = jnp.concatenate(split(owned), axis=0)
    for block in range(4):
        lanes = pl.ds(block * 1024, 1024)
        line = jnp.dot(both, factors_ref[:, lanes], preferred_element_type=F32)
        line = line[:rows] + line[rows:]
        for k in range(8):
            out_ref[block * 8 + k] = line[:, k * 128 : (k + 1) * 128].astype(out_ref.dtype)


def finish_kernel(scale, got_ref, out_ref):
    out_ref[...] = jnp.sum(got_ref[...].astype(F32), axis=0) * scale


def on_device(spectra, pair_first, pair_second, pair_bin, bin_owner):
    blocks = lax.axis_size("blk")
    peers = lax.axis_size("freq")
    sensors, _, freq_dev = spectra.shape
    width = 2 * freq_dev
    slots_each = 2 * NB // blocks
    scale = (F * PAIRS * blocks * blocks / NB) ** (-0.5)
    lists = (pair_first, pair_second, pair_bin)

    part, flat = call(
        power_kernel,
        [shape((peers, 1, sensors), F32), shape((sensors, width), BF16)],
        (spectra.reshape(2 * sensors, freq_dev),), 4, 1_000_000, 300_000,
        scratch=[pltpu.VMEM((2 * sensors, freq_dev), F32)],
    )
    parts = lax.all_to_all(part, "freq", 0, 0, tiled=True)

    anywhere = pl.BlockSpec(memory_space=pl.ANY)
    me = lax.axis_index("freq").astype(jnp.int32).reshape(1)
    factors, rows = call(
        factors_kernel,
        [shape((width, F), BF16), shape((blocks, 4 * CHUNKS, CHUNK), BF16)],
        (me, *lists, part), 8, 10_000_000, 8_000_000,
        specs=[SMEM] + [VMEM] * 3 + [anywhere],
    )

    own, *sent = call(
        white_kernel,
        [shape((sensors, width), BF16)]
        + [shape((sensors + 3 * CHUNKS * len(CARRIED[kind]), width), BF16) for kind in STEPS],
        (parts, flat, rows), 4, 1_000_000, 800_000,
    )

    sent = dict(zip(STEPS, sent))
    held = {"own": own}
    for kind in STEPS:
        hops = [(a, reader(kind, a)) for a in range(blocks)]
        held[kind] = lax.ppermute(sent[kind], "blk", hops)

    acc_shape = shape((NB, width), F32)
    acc = pair_call((("own", "own"),), acc_shape, None, rows, held, None)
    for jobs in (
        (("own", "beside"), ("beside", "own")),
        (("own", "across"), ("across", "beside"), ("beside", "across")),
    ):
        acc = pair_call(jobs, acc_shape, acc, rows, held, None)
    select = call(
        select_kernel, shape((2 * NB, NB), BF16), (bin_owner.reshape(1, NB), acc), 2, 100_000, 30_000,
        specs=[VMEM, anywhere],
    )
    jobs = (("own", "two"), ("across", "two"))
    stacks_shape = shape((blocks, slots_each, width), BF16)
    stacks = pair_call(jobs, stacks_shape, acc, rows, held, select)
    stacks = lax.all_to_all(stacks, "blk", 0, 0, tiled=True)

    line = call(
        lag_kernel, shape((peers, slots_each, freq_dev), BF16), (stacks, factors), 6, 100_000_000, 2_500_000
    )
    line = lax.all_to_all(line, "freq", 0, 0, tiled=True)
    out = call(
        functools.partial(finish_kernel, scale), shape((slots_each, freq_dev), F32), (line,), 2, 100_000, 150_000
    )
    return out.T


def solution(mesh):
    return jax.shard_map(
        on_device,
        mesh=mesh,
        in_specs=(
            P("blk", None, "freq"),
            P("blk", None, None),
            P("blk", None, None),
            P("blk", None, None),
            P(),
        ),
        out_specs=P("freq", "blk"),
        check_vma=False,
    )
```
